32 devices in a mesh: fsdp: 32 (over z, y, x, core).
Axes of the slice: x: 2, y: 2, z: 4, core: 2. Of those that a mesh axis runs over, the one named last changes fastest.
Arguments:
- tokens: bfloat16 [4096, 768], P('fsdp'), may hold values from -6 to 6
- attn_weight: bfloat16 [768, 3072], P(None, 'fsdp')
- w_gate: bfloat16 [768, 3072], P(None, 'fsdp'), may hold values from -0.21875 to 0.21875
- w_up: bfloat16 [768, 3072], P(None, 'fsdp'), may hold values from -0.21875 to 0.21875
- w_down: bfloat16 [3072, 768], P('fsdp'), may hold values from -0.109375 to 0.109375
- norm_gains: float32 [2, 768], replicated, may hold values from 0.5 to 1.5
- bias_table: float32 [32, 12], replicated, may hold values from -4 to 4
- router: float32 [768, 64], replicated, may hold values from -0.4375 to 0.4375
- grad_out: bfloat16 [4096, 768], P('fsdp'), may hold values from -6 to 6
- segment: int32 [4096], P('fsdp'), may hold values from -1 to 7, as said below
- expert_ids: int32 [4096, 2], P('fsdp'), may hold values from 0 to 63, as said below
- bucket_of: int32 [64], replicated, may hold values from 0 to 31, as said below
Outputs:
- result: bfloat16 [4096, 768], P('fsdp')
- grad_tokens: bfloat16 [4096, 768], P('fsdp')
- grad_attn: float32 [768, 3072], P(None, 'fsdp')
- grad_gate: float32 [768, 3072], P(None, 'fsdp')
- grad_up: float32 [768, 3072], P(None, 'fsdp')
- grad_down: float32 [3072, 768], P('fsdp')
- grad_gains: float32 [2, 768], replicated
- grad_table: float32 [32, 12], replicated
- grad_router: float32 [768, 64], replicated
The draws below stay inside these ranges and needn't reach their ends.
Inputs may be any that keep to these rules, and one draw needn't show every extreme that they name: `segment`: each block of 64 slots is one micro-batch of one device; sequences take consecutive slots and are numbered 0 to 7 in order within a block; unused slots, marked -1, come at a block's end; the first block has no unused slot and reaches number 7. `expert_ids`: the two experts of a row differ. `bucket_of`: never falls as the distance grows; equal to the distance below 16.
All inputs are finite; a program needn't handle non-finite values.
Results may differ from the reference program's by a relative error of at most 0.012.
The reference program's roundings to bfloat16 on the way count: a program that leaves them out, or rounds other values in their place, can miss the bound.
Values may be sent and summed in bfloat16 or wider, within the bound.
A program may use at most 192 MiB of HBM per device.

```python
import math
import jax
import jax.numpy as jnp
from jax import lax

D = 768
FF = 3072
ROUTED = 64
HEAD_DIM = 64
HEADS = 12
BUCKETS = 32
MICRO = 2
SLOTS = 64
TOKENS = 4096
N_FSDP = 32


def draw_attn_weight(key, part):
    values = jax.random.normal(key, (D, 4 * D), jnp.float32)
    columns = jnp.arange(4 * D)[None, :]
    scaled = values * jnp.where(columns >= 3 * D, float(D // 8) ** (-0.5), float(D) ** (-0.5))
    return jnp.clip(scaled, -0.6, 0.6).astype(jnp.bfloat16)


def draw_segment(key, part):
    spans = TOKENS // SLOTS
    first_key = jax.random.fold_in(key, 11)
    second_key = jax.random.fold_in(key, 23)
    filled = jax.random.randint(first_key, (spans, 1), SLOTS // 2, SLOTS)
    filled = jnp.where(jnp.arange(spans)[:, None] == 0, SLOTS, filled)
    places = jnp.arange(SLOTS)[None, :]
    starts = jax.random.randint(second_key, (spans, SLOTS), 0, max(4, SLOTS // 4)) == 0
    forced = (places % (SLOTS // 8) == 0) & (jnp.arange(spans)[:, None] == 0)
    starts = jnp.where(places == 0, 0, (starts | forced).astype(jnp.int32))
    numbers = jnp.minimum(jnp.cumsum(starts, axis=1), 7).astype(jnp.int32)
    numbers = jnp.where(places < filled, numbers, -1)
    return numbers.reshape(TOKENS).astype(jnp.int32)


def draw_expert_ids(key, part):
    coin = jax.random.randint(jax.random.fold_in(key, 31), (TOKENS,), 0, 2)
    other_first = jax.random.randint(jax.random.fold_in(key, 37), (TOKENS,), 1, ROUTED)
    first = jnp.where(coin == 0, 0, other_first).astype(jnp.int32)
    rest = jax.random.randint(jax.random.fold_in(key, 41), (TOKENS,), 0, ROUTED - 1)
    second = (rest + (rest >= first).astype(jnp.int32)).astype(jnp.int32)
    swap = jax.random.randint(jax.random.fold_in(key, 43), (TOKENS,), 0, 2)
    left = jnp.where(swap == 0, first, second)
    right = jnp.where(swap == 0, second, first)
    return jnp.stack([left, right], axis=1).astype(jnp.int32)


def draw_bucket_of(key, part):
    places = jnp.arange(SLOTS)
    increments = jax.random.randint(jax.random.fold_in(key, 5), (SLOTS,), 0, 2)
    increments = jnp.where(places < BUCKETS // 2, 1, increments)
    increments = jnp.where(places == 0, 0, increments)
    climbed = jnp.minimum(jnp.cumsum(increments), BUCKETS - 1)
    return jnp.where(places == SLOTS - 1, BUCKETS - 1, climbed).astype(jnp.int32)


def shard_levels(rng, dims, pieces, low, largest):
    loudness, own = 1.0, jax.random.fold_in(rng, 6)
    for position, shards_of in pieces:
        heights = jnp.exp(jax.random.uniform(jax.random.fold_in(own, position), (shards_of,), jnp.float32, low / len(pieces), largest / len(pieces)))
        loudness = loudness * jnp.repeat(heights, dims[position] // shards_of).reshape([-1 if axis == position else 1 for axis in range(len(dims))])
    return loudness


def noise(own_key, extent, width, most, pieces=(), dtype=jnp.bfloat16):
    drawn = width * jax.random.normal(own_key, extent, jnp.float32)
    if pieces:
        drawn = drawn * shard_levels(own_key, extent, pieces, -0.22, 0.18)
    return jnp.clip(drawn, -most, most).astype(dtype)


def setup_inputs(seed: int = 0) -> dict:
    seeds = jax.random.split(jax.random.key(seed), 13)
    tokens = noise(seeds[0], (TOKENS, D), 1.0, 6.0, ((0, 32),))
    attn_weight = draw_attn_weight(jax.random.fold_in(seeds[12], 71), 0)
    w_gate = noise(seeds[2], (D, FF), D ** -0.5, 0.21875, ((1, 32),))
    w_up = noise(seeds[3], (D, FF), D ** -0.5, 0.21875, ((1, 32),))
    w_down = noise(seeds[4], (FF, D), FF ** -0.5, 0.109375, ((0, 32),))
    norm_gains = jnp.clip(1.0 + 0.1 * jax.random.normal(seeds[5], (2, D), jnp.float32), 0.5, 1.5)
    bias_table = noise(seeds[6], (BUCKETS, HEADS), 1.0, 4.0, (), jnp.float32)
    router = noise(seeds[7], (D, ROUTED), (D // 4) ** -0.5, 0.4375, (), jnp.float32)
    grad_out = noise(seeds[8], (TOKENS, D), 1.0, 6.0, ((0, 32),))
    segment = draw_segment(jax.random.fold_in(seeds[12], 71), 0)
    expert_ids = draw_expert_ids(jax.random.fold_in(seeds[12], 71), 0)
    bucket_of = draw_bucket_of(jax.random.fold_in(seeds[12], 71), 0)
    return dict(tokens=tokens, attn_weight=attn_weight, w_gate=w_gate, w_up=w_up, w_down=w_down, norm_gains=norm_gains, bias_table=bias_table, router=router, grad_out=grad_out, segment=segment, expert_ids=expert_ids, bucket_of=bucket_of)


EPSILON = 1e-06
HIGHEST = lax.Precision.HIGHEST

@jax.custom_vjp
def low(v):
    return lax.optimization_barrier(v.astype(jnp.bfloat16)).astype(jnp.float32)

@jax.custom_vjp
def low_back(v):
    return v

def low_keep(v):
    return (low(v), None)

def low_pass(kept, grad):
    return (grad,)

def back_keep(v):
    return (v, None)

def back_low(kept, grad):
    return (low(grad),)
low.defvjp(low_keep, low_pass)
low_back.defvjp(back_keep, back_low)

def matmul_high(left, right):
    return jnp.dot(left, right, precision=HIGHEST)

def attend_span(normed, segments, w_attn, table, bucket_grid):
    triple = low(low_back(matmul_high(normed, w_attn[:, :3 * D])))
    query = triple[:, :D].reshape(SLOTS, HEADS, HEAD_DIM)
    keyset = triple[:, D:2 * D].reshape(SLOTS, HEADS, HEAD_DIM)
    valueset = triple[:, 2 * D:].reshape(SLOTS, HEADS, HEAD_DIM)
    places = jnp.arange(SLOTS)
    allowed = (segments[:, None] == segments[None, :]) & (places[None, :] <= places[:, None])
    offsets = jnp.transpose(table[bucket_grid], (2, 0, 1))
    raw = jnp.einsum('ihd,jhd->hij', query, keyset, precision=HIGHEST)
    scores = low_back(raw * HEAD_DIM ** (-0.5) + offsets)
    weights = jax.nn.softmax(jnp.where(allowed[None], scores, -1e+30), axis=-1)
    mixed = jnp.einsum('hij,jhd->ihd', low(weights), valueset, precision=HIGHEST).reshape(SLOTS, D)
    mixed = low(low_back(mixed))
    return low_back(matmul_high(mixed, w_attn[:, 3 * D:].T))

def forward_group(inputs, segments, choices, w_attn, gate_w, up_w, down_w, gains, table, route, bucket_grid):
    scale_one = lax.rsqrt(lax.optimization_barrier(jnp.mean(inputs * inputs, axis=-1, keepdims=True)) + EPSILON)
    normed = low(inputs * scale_one * gains[0])
    branch = jax.vmap(attend_span, in_axes=(0, 0, None, None, None))(normed, segments, w_attn, table, bucket_grid)
    middle = (inputs + branch).reshape(-1, D)
    scale_two = lax.rsqrt(lax.optimization_barrier(jnp.mean(middle * middle, axis=-1, keepdims=True)) + EPSILON)
    second = low(middle * scale_two * gains[1])
    router_probs = jax.nn.softmax(matmul_high(second, route), axis=-1)
    picked = jnp.any(choices[:, :, None] == jnp.arange(ROUTED)[None, None, :], axis=1)
    picked_f = jnp.where(picked, 1.0, 0.0)
    chosen_total = lax.optimization_barrier(jnp.sum(router_probs * picked_f, axis=-1))
    active = jnp.where(segments.reshape(-1) >= 0, 1.0, 0.0)
    combine = router_probs[:, 0] * picked_f[:, 0] * active / chosen_total
    gated = low_back(matmul_high(second, gate_w))
    lifted = low_back(matmul_high(second, up_w))
    hidden = low(jax.nn.gelu(gated, approximate=True) * lifted)
    expert_out = low_back(matmul_high(hidden, down_w))
    total = middle + combine[:, None] * expert_out
    return total.reshape(inputs.shape)

def reference(tokens, attn_weight, w_gate, w_up, w_down, norm_gains, bias_table, router, grad_out, segment, expert_ids, bucket_of):
    spans = N_FSDP * MICRO
    group = math.gcd(spans, max(1, 4096 // SLOTS))
    places = jnp.arange(SLOTS)
    distance = jnp.maximum(places[:, None] - places[None, :], 0)
    bucket_grid = bucket_of[distance]
    seg_groups = segment.reshape(spans // group, group, SLOTS)
    id_groups = expert_ids.reshape(spans // group, group * SLOTS, 2)

    def forward(inputs, w_attn, gate_w, up_w, down_w, gains, table, route):

        def one_group(items):
            block_inputs, block_segments, block_choices = items
            return forward_group(block_inputs, block_segments, block_choices, w_attn, gate_w, up_w, down_w, gains, table, route, bucket_grid)
        grouped = inputs.reshape(spans // group, group, SLOTS, D)
        outputs = lax.map(jax.checkpoint(one_group), (grouped, seg_groups, id_groups))
        return outputs.reshape(TOKENS, D)
    result, backward = jax.vjp(forward, tokens.astype(jnp.float32), attn_weight.astype(jnp.float32), w_gate.astype(jnp.float32), w_up.astype(jnp.float32), w_down.astype(jnp.float32), norm_gains, bias_table, router)
    grads = backward(grad_out.astype(jnp.float32))
    return (result.astype(jnp.bfloat16), grads[0].astype(jnp.bfloat16), grads[1], grads[2], grads[3], grads[4], grads[5], grads[6], grads[7])
```

```python
import functools
import jax
import jax.numpy as jnp
from jax import lax
from jax.experimental import pallas as pl
from jax.experimental.pallas import tpu as pltpu
from jax.sharding import PartitionSpec as P

EPSILON = 1e-06
HIGHEST = lax.Precision.HIGHEST
MESH = pl.DeviceIdType.MESH
TEAM = 4
F32 = jnp.float32
BF16 = jnp.bfloat16
VMEM = pl.BlockSpec(memory_space=pltpu.VMEM)
ANY = pl.BlockSpec(memory_space=pl.ANY)
CONTRACT_ROWS = (((0,), (0,)), ((), ()))
CONTRACT_COLS = (((1,), (1,)), ((), ()))


def place(n):
    sub = n // (TEAM * TEAM)
    me = lax.axis_index("fsdp")
    p = me // (TEAM * sub)
    t = lax.rem(me // sub, TEAM)
    s = lax.rem(me, sub)
    return sub, p, t, s, (lambda p, t, s: (p * (TEAM * sub) + t * sub + s,))


def greet(peers):
    barrier = pltpu.get_barrier_semaphore()
    for peer in peers:
        pl.semaphore_signal(barrier, inc=1, device_id=peer, device_id_type=MESH)
    pl.semaphore_wait(barrier, len(peers))


def remote(src, dst, send, recv, peer):
    return pltpu.make_async_remote_copy(
        src_ref=src, dst_ref=dst, send_sem=send, recv_sem=recv, device_id=peer, device_id_type=MESH
    )


def other(index, step, count):
    return lax.rem(index + step, count)


def gather_kernel(n, w_ref, tok_ref, dy_ref, meta_ref, w_all, tok_all, dy_all, meta_all,
                  p_send, p_recv, s_send, s_recv, t_send, t_recv, own_sem):
    sub, p, t, s, dev = place(n)
    peers = [dev(other(p, k, TEAM), t, s) for k in range(1, TEAM)]
    peers += [dev(p, t, other(s, k, sub)) for k in range(1, sub)]
    peers += [dev(p, other(t, k, TEAM), s) for k in range(1, TEAM)]
    greet(peers)
    copies = []
    for k in range(1, TEAM):
        c = remote(w_ref, w_all.at[:, p, s], p_send.at[k], p_recv.at[k], dev(other(p, k, TEAM), t, s))
        c.start()
        copies.append(c)
    for k in range(1, sub):
        c = remote(w_ref, w_all.at[:, p, s], s_send.at[0, k], s_recv.at[0, k], dev(p, t, other(s, k, sub)))
        c.start()
        copies.append(c)
    for i, (src, dst) in enumerate(((tok_ref, tok_all), (dy_ref, dy_all), (meta_ref, meta_all))):
        for k in range(1, TEAM):
            c = remote(src, dst.at[t], t_send.at[i, k], t_recv.at[i, k], dev(p, other(t, k, TEAM), s))
            c.start()
            copies.append(c)
    local = [pltpu.make_async_copy(w_ref, w_all.at[:, p, s], own_sem.at[0]),
             pltpu.make_async_copy(tok_ref, tok_all.at[t], own_sem.at[1]),
             pltpu.make_async_copy(dy_ref, dy_all.at[t], own_sem.at[2]),
             pltpu.make_async_copy(meta_ref, meta_all.at[t], own_sem.at[3])]
    for c in local:
        c.start()
    for k in range(1, TEAM):
        copies[k - 1].wait_recv()
        q = other(p, TEAM - k, TEAM)
        for j in range(1, sub):
            c = remote(w_all.at[:, q, s], w_all.at[:, q, s], s_send.at[k, j], s_recv.at[k, j],
                       dev(p, t, other(s, j, sub)))
            c.start()
            copies.append(c)
    for k in range(1, TEAM):
        copies[k - 1].wait_send()
    for c in copies[TEAM - 1:]:
        c.wait()
    for c in local:
        c.wait()


def gather(n, w, tok, dy, meta):
    sub = n // (TEAM * TEAM)
    dma = pltpu.SemaphoreType.DMA
    shape = jax.ShapeDtypeStruct
    return pl.pallas_call(
        functools.partial(gather_kernel, n),
        out_shape=(
            shape((w.shape[0], TEAM, sub) + w.shape[1:], BF16),
            shape((TEAM,) + tok.shape, BF16),
            shape((TEAM,) + dy.shape, BF16),
            shape((TEAM,) + meta.shape, jnp.int32),
        ),
        in_specs=[VMEM] * 4,
        out_specs=(ANY,) * 4,
        scratch_shapes=[dma((TEAM,)), dma((TEAM,)), dma((TEAM, sub)), dma((TEAM, sub)),
                        dma((3, TEAM)), dma((3, TEAM)), dma((4,))],
        compiler_params=pltpu.CompilerParams(collective_id=0, has_side_effects=True),
        name="gather_all",
    )(w, tok, dy, meta)


def middle_kernel(n, part_ref, x_ref, gain_ref, y_ref, h_all, got, held, a_send, a_recv, b_send, b_recv, own_sem):
    sub, p, t, s, dev = place(n)
    peers = [dev(p, other(t, k, TEAM), s) for k in range(1, TEAM)]
    greet(peers)
    copies = []
    for k in range(1, TEAM):
        u = other(t, k, TEAM)
        c = remote(part_ref.at[u], got.at[k - 1], a_send.at[k], a_recv.at[k], dev(p, u, s))
        c.start()
        copies.append(c)
    total = x_ref[...].astype(F32) + part_ref[t].astype(F32)
    for k in range(1, TEAM):
        copies[k - 1].wait_recv()
        total = total + got[k - 1].astype(F32)
    y_ref[...] = total
    scale = lax.rsqrt(jnp.mean(total * total, axis=-1, keepdims=True) + EPSILON)
    held[...] = (total * scale * gain_ref[1:2, :]).astype(BF16)
    local = pltpu.make_async_copy(held, h_all.at[t], own_sem)
    local.start()
    sends = []
    for k in range(1, TEAM):
        c = remote(held, h_all.at[t], b_send.at[k], b_recv.at[k], dev(p, other(t, k, TEAM), s))
        c.start()
        sends.append(c)
    for c in copies:
        c.wait_send()
    for c in sends:
        c.wait()
    local.wait()


def middle_exchange(n, part, x, gains):
    dma = pltpu.SemaphoreType.DMA
    shape = jax.ShapeDtypeStruct
    return pl.pallas_call(
        functools.partial(middle_kernel, n),
        out_shape=(shape(x.shape, F32), shape((TEAM,) + x.shape, BF16)),
        in_specs=[VMEM] * 3,
        out_specs=(VMEM, ANY),
        scratch_shapes=[pltpu.VMEM((TEAM - 1,) + x.shape, BF16), pltpu.VMEM(x.shape, BF16),
                        dma((TEAM,)), dma((TEAM,)), dma((TEAM,)), dma((TEAM,)), dma],
        compiler_params=pltpu.CompilerParams(collective_id=1, has_side_effects=True),
        name="middle_exchange",
    )(part, x, gains)


def reduce_kernel(n, m, *refs):
    parts, grad_ref = refs[:m], refs[m]
    outs, grad_out = refs[m + 1:2 * m + 1], refs[2 * m + 1]
    (got, sib, to_send, far, t_send, t_recv, s_send, s_recv, p_send, p_recv) = refs[2 * m + 2:]
    sub, p, t, s, dev = place(n)
    peers = [dev(other(p, k, TEAM), t, s) for k in range(1, TEAM)]
    peers += [dev(p, t, other(s, k, sub)) for k in range(1, sub)]
    peers += [dev(p, other(t, k, TEAM), s) for k in range(1, TEAM)]
    greet(peers)
    kinds = grad_ref.shape[0]
    near, tokens, wide = [], [], []
    for k in range(1, sub):
        v = other(s, k, sub)
        c = remote(grad_ref.at[:, :, v], sib.at[k - 1], s_send.at[k], s_recv.at[k], dev(p, t, v))
        c.start()
        near.append(c)
    for i in range(m):
        for k in range(1, TEAM):
            u = other(t, k, TEAM)
            c = remote(parts[i].at[u], got.at[i, k - 1], t_send.at[i, k], t_recv.at[i, k], dev(p, u, s))
            c.start()
            tokens.append(c)
    for c in near:
        c.wait_recv()
    for k in range(1, TEAM):
        q = other(p, k, TEAM)

        def fold(kind, carry, q=q, k=k):
            total = grad_ref[kind, q, s].astype(F32)
            for j in range(1, sub):
                total = total + sib[j - 1, kind, q].astype(F32)
            to_send[k - 1, kind] = total.astype(BF16)
            return carry

        lax.fori_loop(0, kinds, fold, 0)
        c = remote(to_send.at[k - 1], far.at[k - 1], p_send.at[k], p_recv.at[k], dev(q, t, s))
        c.start()
        wide.append(c)
    for i in range(m):
        total = parts[i][t].astype(F32)
        for k in range(1, TEAM):
            tokens[i * (TEAM - 1) + k - 1].wait_recv()
            total = total + got[i, k - 1].astype(F32)
        outs[i][...] = total
    for c in wide:
        c.wait_recv()

    def finish(kind, carry):
        total = grad_ref[kind, p, s].astype(F32)
        for j in range(1, sub):
            total = total + sib[j - 1, kind, p].astype(F32)
        for k in range(1, TEAM):
            total = total + far[k - 1, kind].astype(F32)
        grad_out[kind] = total
        return carry

    lax.fori_loop(0, kinds, finish, 0)
    for c in near + tokens + wide:
        c.wait_send()


def reduce_exchange(n, parts, grads, ident):
    sub = n // (TEAM * TEAM)
    m = len(parts)
    dma = pltpu.SemaphoreType.DMA
    shape = jax.ShapeDtypeStruct
    block = parts[0].shape[1:]
    kinds, tile = grads.shape[0], grads.shape[3:]
    outs = pl.pallas_call(
        functools.partial(reduce_kernel, n, m),
        out_shape=(shape(block, F32),) * m + (shape((kinds,) + tile, F32),),
        in_specs=[VMEM] * (m + 1),
        out_specs=(VMEM,) * (m + 1),
        scratch_shapes=[
            pltpu.VMEM((m, TEAM - 1) + block, BF16),
            pltpu.VMEM((sub - 1, kinds, TEAM) + tile, BF16),
            pltpu.VMEM((TEAM - 1, kinds) + tile, BF16),
            pltpu.VMEM((TEAM - 1, kinds) + tile, BF16),
            dma((m, TEAM)), dma((m, TEAM)), dma((sub,)), dma((sub,)), dma((TEAM,)), dma((TEAM,)),
        ],
        compiler_params=pltpu.CompilerParams(collective_id=ident, has_side_effects=True),
        name=f"reduce_{ident}",
    )(*parts, grads)
    return outs[:m], outs[m]


def share_kernel(n, x_ref, out, send, recv, own_sem):
    sub, p, t, s, dev = place(n)
    peers = [dev(p, other(t, k, TEAM), s) for k in range(1, TEAM)]
    greet(peers)
    local = pltpu.make_async_copy(x_ref, out.at[t], own_sem)
    local.start()
    copies = []
    for k in range(1, TEAM):
        c = remote(x_ref, out.at[t], send.at[k], recv.at[k], peers[k - 1])
        c.start()
        copies.append(c)
    for c in copies:
        c.wait()
    local.wait()


def share(n, x):
    dma = pltpu.SemaphoreType.DMA
    return pl.pallas_call(
        functools.partial(share_kernel, n),
        out_shape=jax.ShapeDtypeStruct((TEAM,) + x.shape, x.dtype),
        in_specs=[VMEM],
        out_specs=ANY,
        scratch_shapes=[dma((TEAM,)), dma((TEAM,)), dma],
        compiler_params=pltpu.CompilerParams(collective_id=3, has_side_effects=True),
        name="share_rows",
    )(x)


def small_kernel(n, x_ref, out_ref, got, mine, far, a_send, a_recv, b_send, b_recv, c_send, c_recv):
    sub, p, t, s, dev = place(n)
    team = [dev(p, other(t, k, TEAM), s) for k in range(1, TEAM)]
    count = TEAM * sub
    own = p * sub + s
    ring = []
    for k in range(1, count):
        v = other(own, k, count)
        ring.append(dev(v // sub, t, lax.rem(v, sub)))
    greet(team + ring)
    first, second, third = [], [], []
    for k in range(1, TEAM):
        c = remote(x_ref.at[other(t, k, TEAM)], got.at[k - 1], a_send.at[k], a_recv.at[k], team[k - 1])
        c.start()
        first.append(c)
    total = x_ref[t]
    for k in range(1, TEAM):
        first[k - 1].wait_recv()
        total = total + got[k - 1]
    mine[...] = total
    for k in range(1, count):
        c = remote(mine, far.at[own], b_send.at[k], b_recv.at[k], ring[k - 1])
        c.start()
        second.append(c)
    far[own] = total
    for c in second:
        c.wait_recv()
    summed = far[0]
    for k in range(1, count):
        summed = summed + far[k]
    out_ref[t] = summed
    for k in range(1, TEAM):
        c = remote(out_ref.at[t], out_ref.at[t], c_send.at[k], c_recv.at[k], team[k - 1])
        c.start()
        third.append(c)
    for c in first + second:
        c.wait_send()
    for c in third:
        c.wait()


def small_sum(n, x):
    count = n // TEAM
    dma = pltpu.SemaphoreType.DMA
    tile = x.shape[1:]
    return pl.pallas_call(
        functools.partial(small_kernel, n),
        out_shape=jax.ShapeDtypeStruct(x.shape, F32),
        in_specs=[VMEM],
        out_specs=VMEM,
        scratch_shapes=[pltpu.VMEM((TEAM - 1,) + tile, F32), pltpu.VMEM(tile, F32), pltpu.VMEM((count,) + tile, F32),
                        dma((TEAM,)), dma((TEAM,)), dma((count,)), dma((count,)), dma((TEAM,)), dma((TEAM,))],
        compiler_params=pltpu.CompilerParams(collective_id=5, has_side_effects=True),
        name="small_sum",
    )(x)


def gelu_tanh(inner):
    return jax.nn.gelu(inner, approximate=True)


def norm_back(inputs, scale, gain, upstream):
    weighted = gain * upstream
    return scale * weighted - inputs * scale * scale * scale * jnp.mean(
        weighted * inputs, axis=-1, keepdims=True
    )


def dot_t(a, b):
    return lax.dot_general(a, b, CONTRACT_COLS, preferred_element_type=F32)


def dot_r(a, b):
    return lax.dot_general(a, b, CONTRACT_ROWS, preferred_element_type=F32)


def dot(a, b):
    return jnp.dot(a, b, preferred_element_type=F32)


def body(n, tokens, attn_weight, w_gate, w_up, w_down, norm_gains, bias_table, router,
         grad_out, segment, expert_ids, bucket_of):
    rows, width = tokens.shape
    slots = bucket_of.shape[0]
    routed = router.shape[1]
    buckets, head_count = bias_table.shape
    head_width = width // head_count
    factor = head_width ** (-0.5)
    heads = head_count // TEAM
    part = heads * head_width
    sub, _, t, _, _ = place(n)
    all_rows = TEAM * rows
    spans = all_rows // slots

    w_local = jnp.stack([attn_weight.T, w_gate.T, w_up.T, w_down])
    meta = jnp.concatenate([segment[None], expert_ids.T, jnp.zeros((5, rows), jnp.int32)], axis=0)
    w_all, tok_all, dy_all, meta_all = gather(n, w_local, tokens, grad_out, meta)
    w_all = w_all.reshape(4, -1, width)
    attn_t, gate_t, up_t, down = w_all[0], w_all[1], w_all[2], w_all[3]
    qkv_t, out_t = attn_t[: 3 * part], attn_t[3 * part :]
    inputs = tok_all.reshape(all_rows, width).astype(F32)
    segments = meta_all[:, 0, :].reshape(all_rows)
    id_a = meta_all[:, 1, :].reshape(all_rows)
    id_b = meta_all[:, 2, :].reshape(all_rows)

    places = jnp.arange(slots)
    gap = places[:, None] - places[None, :]
    causal = gap >= 0
    gap_hit = (gap[:, :, None] == places[None, None, :]).astype(F32)
    bucket_hit = (bucket_of[:, None] == jnp.arange(buckets)[None, :]).astype(F32)
    table_mine = lax.dynamic_slice(bias_table, (0, heads * t), (buckets, heads))
    by_gap = jnp.dot(bucket_hit, table_mine, precision=HIGHEST)
    offsets = jnp.einsum("ijd,dh->hij", gap_hit, by_gap, precision=HIGHEST)

    scale_one = lax.rsqrt(jnp.mean(inputs * inputs, axis=-1, keepdims=True) + EPSILON)
    normed = (inputs * scale_one * norm_gains[0]).astype(BF16)
    triple = dot_t(normed, qkv_t).astype(BF16)
    heads_of = lambda v: v.reshape(spans, slots, heads, head_width)
    query = heads_of(triple[:, :part])
    keyset = heads_of(triple[:, part : 2 * part])
    valueset = heads_of(triple[:, 2 * part :])
    seg = segments.reshape(spans, slots)
    allowed = (seg[:, :, None] == seg[:, None, :]) & causal[None]
    raw = jnp.einsum("bihd,bjhd->bhij", query, keyset, preferred_element_type=F32)
    scores = jnp.where(allowed[:, None], raw * factor + offsets[None], -1e30)
    peak = jnp.max(scores, axis=-1, keepdims=True)
    lifted_scores = jnp.exp(scores - peak)
    weights = lifted_scores / jnp.sum(lifted_scores, axis=-1, keepdims=True)
    weights_low = weights.astype(BF16)
    mixed = jnp.einsum("bhij,bjhd->bihd", weights_low, valueset, preferred_element_type=F32)
    mixed = mixed.reshape(all_rows, part).astype(BF16)
    branch = dot(mixed, out_t).astype(BF16).reshape(TEAM, rows, width)
    middle, second_all = middle_exchange(n, branch, tokens, norm_gains)
    second_all = second_all.reshape(all_rows, width)

    second_wide = second_all.astype(F32)
    probs_all = jax.nn.softmax(jnp.dot(second_wide, router, precision=HIGHEST), axis=-1)
    lanes = jnp.arange(routed)[None, :]
    picked_all = jnp.where((id_a[:, None] == lanes) | (id_b[:, None] == lanes), 1.0, 0.0)
    total_all = jnp.sum(probs_all * picked_all, axis=-1)
    live_all = picked_all[:, 0] * jnp.where(segments >= 0, 1.0, 0.0)
    combine_all = probs_all[:, 0] * live_all / total_all
    gated = dot_t(second_all, gate_t)
    lifted = dot_t(second_all, up_t)
    activated, gelu_back = jax.vjp(gelu_tanh, gated)
    hidden = (activated * lifted).astype(BF16)
    out_part = dot(hidden, down).astype(BF16).reshape(TEAM, rows, width)
    d_expert = (combine_all[:, None] * dy_all.reshape(all_rows, width).astype(F32)).astype(BF16)
    d_hidden = dot_t(d_expert, down)
    d_gated = gelu_back(d_hidden * lifted)[0].astype(BF16)
    d_lifted = (d_hidden * activated).astype(BF16)
    back_part = (dot(d_gated, gate_t) + dot(d_lifted, up_t)).astype(BF16).reshape(TEAM, rows, width)
    grad_ffn = jnp.stack(
        [dot_r(d_gated, second_all).astype(BF16), dot_r(d_lifted, second_all).astype(BF16),
         dot_r(hidden, d_expert).astype(BF16)]
    ).reshape(3, TEAM, sub, -1, width)
    (expert_out, d_second), g_ffn = reduce_exchange(n, (out_part, back_part), grad_ffn, 2)

    mine = lambda v: lax.dynamic_slice_in_dim(v, t * rows, rows, 0)
    second, probs, picked = mine(second_wide), mine(probs_all), mine(picked_all)
    chosen_total, live, combine = mine(total_all), mine(live_all), mine(combine_all)
    upstream = grad_out.astype(F32)
    result = (middle + combine[:, None] * expert_out).astype(BF16)
    d_combine = jnp.sum(expert_out * upstream, axis=-1)
    first_hot = jnp.where(jnp.arange(routed) == 0, 1.0, 0.0)
    ratio = probs[:, 0] / (chosen_total * chosen_total)
    d_probs = (d_combine * live)[:, None] * (
        first_hot[None, :] / chosen_total[:, None] - ratio[:, None] * picked
    )
    d_logits = probs * (d_probs - jnp.sum(d_probs * probs, axis=-1, keepdims=True))
    grad_router_t = lax.dot_general(d_logits, second, CONTRACT_ROWS, precision=HIGHEST)
    d_second = d_second + jnp.dot(d_logits, router.T, precision=HIGHEST)
    scale_two = lax.rsqrt(jnp.mean(middle * middle, axis=-1, keepdims=True) + EPSILON)
    gain_two = jnp.sum(d_second * middle * scale_two, axis=0)
    d_middle = upstream + norm_back(middle, scale_two, norm_gains[1], d_second)
    d_branch = share(n, d_middle.astype(BF16)).reshape(all_rows, width)

    grad_out_t = dot_r(mixed, d_branch)
    d_mixed = heads_of(dot_t(d_branch, out_t).astype(BF16))
    d_weights = jnp.einsum("bihd,bjhd->bhij", d_mixed, valueset, preferred_element_type=F32)
    d_values = jnp.einsum("bhij,bihd->bjhd", weights_low, d_mixed, preferred_element_type=F32)
    d_scores = weights * (d_weights - jnp.sum(weights * d_weights, axis=-1, keepdims=True))
    d_scores = d_scores.astype(BF16)
    d_query = jnp.einsum("bhij,bjhd->bihd", d_scores, keyset, preferred_element_type=F32) * factor
    d_keys = jnp.einsum("bhij,bihd->bjhd", d_scores, query, preferred_element_type=F32) * factor
    score_sum = jnp.sum(d_scores.astype(F32), axis=0)
    gap_sum = jnp.einsum("hij,ijd->dh", score_sum, gap_hit, precision=HIGHEST)
    table_part = lax.dot_general(bucket_hit, gap_sum, CONTRACT_ROWS, precision=HIGHEST)
    grad_table = lax.dynamic_update_slice(jnp.zeros(bias_table.shape, F32), table_part, (0, heads * t))
    flat = lambda v: v.reshape(all_rows, part).astype(BF16)
    d_triple = jnp.concatenate([flat(d_query), flat(d_keys), flat(d_values)], axis=1)
    grad_in_t = dot_r(d_triple, normed)
    grad_attn = jnp.concatenate([grad_in_t, grad_out_t], axis=0).astype(BF16)
    grad_attn = grad_attn.reshape(1, TEAM, sub, -1, width)
    d_normed_part = dot(d_triple, qkv_t).astype(BF16).reshape(TEAM, rows, width)
    (d_normed,), g_attn = reduce_exchange(n, (d_normed_part,), grad_attn, 4)

    own_inputs = tokens.astype(F32)
    own_scale = mine(scale_one)
    gain_one = jnp.sum(d_normed * own_inputs * own_scale, axis=0)
    input_grad = (d_middle + norm_back(own_inputs, own_scale, norm_gains[0], d_normed)).astype(BF16)
    table_flat = grad_table.reshape(-1)
    lines = -(-table_flat.shape[0] // width)
    table_rows = jnp.pad(table_flat, (0, lines * width - table_flat.shape[0])).reshape(lines, width)
    small = jnp.concatenate([grad_router_t, gain_one[None], gain_two[None], table_rows], axis=0)
    depth = -(-small.shape[0] // (8 * TEAM)) * 8
    small = jnp.pad(small, ((0, depth * TEAM - small.shape[0]), (0, 0))).reshape(TEAM, depth, width)
    small = small_sum(n, small).reshape(TEAM * depth, width)
    grad_router = small[:routed].T
    grad_gains = small[routed : routed + 2]
    grad_table = small[routed + 2 : routed + 2 + lines].reshape(-1)[: table_flat.shape[0]].reshape(bias_table.shape)
    return (result, input_grad, g_attn[0].T, g_ffn[0].T, g_ffn[1].T, g_ffn[2],
            grad_gains, grad_table, grad_router)


def solution(mesh):
    n = mesh.shape["fsdp"]
    row, col = P("fsdp", None), P(None, "fsdp")
    in_specs = (row, col, col, col, row, P(), P(), P(), row, P("fsdp"), row, P())
    out_specs = (row, row, col, col, col, row, P(), P(), P())
    return jax.shard_map(
        functools.partial(body, n), mesh=mesh, in_specs=in_specs, out_specs=out_specs, check_vma=False
    )
```

```python
import functools
import jax
import jax.numpy as jnp
from jax import lax
from jax.experimental import pallas as pl
from jax.experimental.pallas import tpu as pltpu
from jax.sharding import PartitionSpec as P

EPSILON = 1e-06
HIGHEST = lax.Precision.HIGHEST
MESH = pl.DeviceIdType.MESH
TEAM = 4
F32 = jnp.float32
BF16 = jnp.bfloat16
VMEM = pl.BlockSpec(memory_space=pltpu.VMEM)
ANY = pl.BlockSpec(memory_space=pl.ANY)
CONTRACT_ROWS = (((0,), (0,)), ((), ()))
CONTRACT_COLS = (((1,), (1,)), ((), ()))


def place(n):
    sub = n // (TEAM * TEAM)
    me = lax.axis_index("fsdp")
    p = me // (TEAM * sub)
    t = lax.rem(me // sub, TEAM)
    s = lax.rem(me, sub)
    return sub, p, t, s, (lambda p, t, s: (p * (TEAM * sub) + t * sub + s,))


def greet(peers):
    barrier = pltpu.get_barrier_semaphore()
    for peer in peers:
        pl.semaphore_signal(barrier, inc=1, device_id=peer, device_id_type=MESH)
    pl.semaphore_wait(barrier, len(peers))


def remote(src, dst, send, recv, peer):
    return pltpu.make_async_remote_copy(
        src_ref=src, dst_ref=dst, send_sem=send, recv_sem=recv, device_id=peer, device_id_type=MESH
    )


def other(index, step, count):
    return lax.rem(index + step, count)


def spread_peers(sub, p, t, s, dev):
    peers = [dev(other(p, k, TEAM), t, s) for k in range(1, TEAM)]
    return peers + [dev(p, t, other(s, k, sub)) for k in range(1, sub)]


def team_peers(p, t, s, dev):
    return [dev(p, other(t, k, TEAM), s) for k in range(1, TEAM)]


def weights_start(n, w_ref, w_all, sems):
    sub, p, t, s, dev = place(n)
    p_send, p_recv, s_send, s_recv, own_sem = sems
    wide, near, local = [], [], []
    for i in range(w_ref.shape[0]):
        for k in range(1, TEAM):
            c = remote(w_ref.at[i], w_all.at[i, p, s], p_send.at[i, k], p_recv.at[i, k],
                       dev(other(p, k, TEAM), t, s))
            c.start()
            wide.append(c)
    for i in range(w_ref.shape[0]):
        for k in range(1, sub):
            c = remote(w_ref.at[i], w_all.at[i, p, s], s_send.at[i, 0, k], s_recv.at[i, 0, k],
                       dev(p, t, other(s, k, sub)))
            c.start()
            near.append(c)
        c = pltpu.make_async_copy(w_ref.at[i], w_all.at[i, p, s], own_sem.at[i])
        c.start()
        local.append(c)
    return wide, near, local


def weights_finish(n, w_all, sems, state):
    sub, p, t, s, dev = place(n)
    _, _, s_send, s_recv, _ = sems
    wide, near, local = state
    for i in range(w_all.shape[0]):
        for k in range(1, TEAM):
            wide[i * (TEAM - 1) + k - 1].wait_recv()
            q = other(p, TEAM - k, TEAM)
            for j in range(1, sub):
                c = remote(w_all.at[i, q, s], w_all.at[i, q, s], s_send.at[i, k, j], s_recv.at[i, k, j],
                           dev(p, t, other(s, j, sub)))
                c.start()
                near.append(c)
    for c in wide:
        c.wait_send()
    for c in near:
        c.wait()
    for c in local:
        c.wait()


def weights_sems(n, kinds):
    sub = n // (TEAM * TEAM)
    dma = pltpu.SemaphoreType.DMA
    return [dma((kinds, TEAM)), dma((kinds, TEAM)), dma((kinds, TEAM, sub)), dma((kinds, TEAM, sub)), dma((kinds,))]


def weights_shape(n, w):
    return jax.ShapeDtypeStruct((w.shape[0], TEAM, n // (TEAM * TEAM)) + w.shape[1:], w.dtype)


def gather_kernel(n, w_ref, tok_ref, dy_ref, meta_ref, w_all, tok_all, dy_all, meta_all,
                  t_send, t_recv, own_sem, *sems):
    sub, p, t, s, dev = place(n)
    greet(spread_peers(sub, p, t, s, dev) + team_peers(p, t, s, dev))
    state = weights_start(n, w_ref, w_all, sems)
    copies, local = [], []
    for i, (src, dst) in enumerate(((tok_ref, tok_all), (dy_ref, dy_all), (meta_ref, meta_all))):
        for k in range(1, TEAM):
            c = remote(src, dst.at[t], t_send.at[i, k], t_recv.at[i, k], dev(p, other(t, k, TEAM), s))
            c.start()
            copies.append(c)
        c = pltpu.make_async_copy(src, dst.at[t], own_sem.at[i])
        c.start()
        local.append(c)
    weights_finish(n, w_all, sems, state)
    for c in copies:
        c.wait()
    for c in local:
        c.wait()


def gather(n, w, tok, dy, meta):
    dma = pltpu.SemaphoreType.DMA
    shape = jax.ShapeDtypeStruct
    return pl.pallas_call(
        functools.partial(gather_kernel, n),
        out_shape=(
            weights_shape(n, w),
            shape((TEAM,) + tok.shape, BF16),
            shape((TEAM,) + dy.shape, BF16),
            shape((TEAM,) + meta.shape, jnp.int32),
        ),
        in_specs=[VMEM] * 4,
        out_specs=(ANY,) * 4,
        scratch_shapes=[dma((3, TEAM)), dma((3, TEAM)), dma((3,))] + weights_sems(n, w.shape[0]),
        compiler_params=pltpu.CompilerParams(collective_id=0, has_side_effects=True),
        name="gather_all",
    )(w, tok, dy, meta)


def middle_kernel(n, part_ref, x_ref, gain_ref, w_ref, y_ref, h_all, w_all, got, held,
                  a_send, a_recv, b_send, b_recv, own_sem, *sems):
    sub, p, t, s, dev = place(n)
    greet(spread_peers(sub, p, t, s, dev) + team_peers(p, t, s, dev))
    copies = []
    for k in range(1, TEAM):
        u = other(t, k, TEAM)
        c = remote(part_ref.at[u], got.at[k - 1], a_send.at[k], a_recv.at[k], dev(p, u, s))
        c.start()
        copies.append(c)
    state = weights_start(n, w_ref, w_all, sems)
    total = x_ref[...].astype(F32) + part_ref[t].astype(F32)
    for k in range(1, TEAM):
        copies[k - 1].wait_recv()
        total = total + got[k - 1].astype(F32)
    y_ref[...] = total
    scale = lax.rsqrt(jnp.mean(total * total, axis=-1, keepdims=True) + EPSILON)
    held[...] = (total * scale * gain_ref[1:2, :]).astype(BF16)
    local = pltpu.make_async_copy(held, h_all.at[t], own_sem)
    local.start()
    sends = []
    for k in range(1, TEAM):
        c = remote(held, h_all.at[t], b_send.at[k], b_recv.at[k], dev(p, other(t, k, TEAM), s))
        c.start()
        sends.append(c)
    weights_finish(n, w_all, sems, state)
    for c in copies:
        c.wait_send()
    for c in sends:
        c.wait()
    local.wait()


def middle_exchange(n, part, x, gains, w):
    dma = pltpu.SemaphoreType.DMA
    shape = jax.ShapeDtypeStruct
    return pl.pallas_call(
        functools.partial(middle_kernel, n),
        out_shape=(shape(x.shape, F32), shape((TEAM,) + x.shape, BF16), weights_shape(n, w)),
        in_specs=[VMEM] * 4,
        out_specs=(VMEM, ANY, ANY),
        scratch_shapes=[pltpu.VMEM((TEAM - 1,) + x.shape, BF16), pltpu.VMEM(x.shape, BF16),
                        dma((TEAM,)), dma((TEAM,)), dma((TEAM,)), dma((TEAM,)), dma] + weights_sems(n, w.shape[0]),
        compiler_params=pltpu.CompilerParams(collective_id=1, has_side_effects=True),
        name="middle_exchange",
    )(part, x, gains, w)


def reduce_kernel(n, m, h, *refs):
    parts, rows, grad_ref = refs[:m], refs[m:m + h], refs[m + h]
    refs = refs[m + h + 1:]
    outs, rows_all, grad_out = refs[:m], refs[m:m + h], refs[m + h]
    (got, sib, to_send, far, t_send, t_recv, h_send, h_recv, own_sem,
     s_send, s_recv, p_send, p_recv) = refs[m + h + 1:]
    sub, p, t, s, dev = place(n)
    greet(spread_peers(sub, p, t, s, dev) + team_peers(p, t, s, dev))
    kinds = grad_ref.shape[0]
    near, tokens, wide, shared, local = [], [], [], [], []
    for kind in range(kinds):
        for k in range(1, sub):
            v = other(s, k, sub)
            c = remote(grad_ref.at[kind, :, v], sib.at[kind, k - 1], s_send.at[kind, k], s_recv.at[kind, k],
                       dev(p, t, v))
            c.start()
            near.append(c)
    for i in range(h):
        for k in range(1, TEAM):
            c = remote(rows[i], rows_all[i].at[t], h_send.at[i, k], h_recv.at[i, k],
                       dev(p, other(t, k, TEAM), s))
            c.start()
            shared.append(c)
        c = pltpu.make_async_copy(rows[i], rows_all[i].at[t], own_sem.at[i])
        c.start()
        local.append(c)
    for i in range(m):
        for k in range(1, TEAM):
            u = other(t, k, TEAM)
            c = remote(parts[i].at[u], got.at[i, k - 1], t_send.at[i, k], t_recv.at[i, k], dev(p, u, s))
            c.start()
            tokens.append(c)
    for kind in range(kinds):
        for c in near[kind * (sub - 1):(kind + 1) * (sub - 1)]:
            c.wait_recv()
        for k in range(1, TEAM):
            q = other(p, k, TEAM)
            total = grad_ref[kind, q, s].astype(F32)
            for j in range(1, sub):
                total = total + sib[kind, j - 1, q].astype(F32)
            to_send[kind, k - 1] = total.astype(BF16)
            c = remote(to_send.at[kind, k - 1], far.at[kind, k - 1], p_send.at[kind, k], p_recv.at[kind, k],
                       dev(q, t, s))
            c.start()
            wide.append(c)
    for i in range(m):
        total = parts[i][t].astype(F32)
        for k in range(1, TEAM):
            tokens[i * (TEAM - 1) + k - 1].wait_recv()
            total = total + got[i, k - 1].astype(F32)
        outs[i][...] = total
    for kind in range(kinds):
        for c in wide[kind * (TEAM - 1):(kind + 1) * (TEAM - 1)]:
            c.wait_recv()
        total = grad_ref[kind, p, s].astype(F32)
        for j in range(1, sub):
            total = total + sib[kind, j - 1, p].astype(F32)
        for k in range(1, TEAM):
            total = total + far[kind, k - 1].astype(F32)
        grad_out[kind] = total
    for c in near + tokens + wide:
        c.wait_send()
    for c in shared:
        c.wait()
    for c in local:
        c.wait()


def reduce_exchange(n, parts, rows, grads, ident):
    sub = n // (TEAM * TEAM)
    m, h = len(parts), len(rows)
    dma = pltpu.SemaphoreType.DMA
    shape = jax.ShapeDtypeStruct
    block = parts[0].shape[1:] if m else (8, 128)
    kinds, tile = grads.shape[0], grads.shape[3:]
    outs = pl.pallas_call(
        functools.partial(reduce_kernel, n, m, h),
        out_shape=(shape(block, F32),) * m
        + tuple(shape((TEAM,) + v.shape, v.dtype) for v in rows)
        + (shape((kinds,) + tile, F32),),
        in_specs=[VMEM] * (m + h + 1),
        out_specs=(VMEM,) * m + (ANY,) * h + (VMEM,),
        scratch_shapes=[
            pltpu.VMEM((max(m, 1), TEAM - 1) + block, BF16),
            pltpu.VMEM((kinds, sub - 1, TEAM) + tile, BF16),
            pltpu.VMEM((kinds, TEAM - 1) + tile, BF16),
            pltpu.VMEM((kinds, TEAM - 1) + tile, BF16),
            dma((max(m, 1), TEAM)), dma((max(m, 1), TEAM)),
            dma((max(h, 1), TEAM)), dma((max(h, 1), TEAM)), dma((max(h, 1),)),
            dma((kinds, sub)), dma((kinds, sub)), dma((kinds, TEAM)), dma((kinds, TEAM)),
        ],
        compiler_params=pltpu.CompilerParams(collective_id=ident, has_side_effects=True),
        name=f"reduce_{ident}",
    )(*parts, *rows, grads)
    return outs[:m], outs[m:m + h], outs[m + h]


def small_kernel(n, x_ref, out_ref, got, mine, sib, held, far,
                 a_send, a_recv, s_send, s_recv, b_send, b_recv, c_send, c_recv):
    sub, p, t, s, dev = place(n)
    greet(spread_peers(sub, p, t, s, dev) + team_peers(p, t, s, dev))
    first, near, second, third = [], [], [], []
    for k in range(1, TEAM):
        u = other(t, k, TEAM)
        c = remote(x_ref.at[u], got.at[k - 1], a_send.at[k], a_recv.at[k], dev(p, u, s))
        c.start()
        first.append(c)
    total = x_ref[t]
    for k in range(1, TEAM):
        first[k - 1].wait_recv()
        total = total + got[k - 1]
    mine[...] = total
    sib[s] = total
    for k in range(1, sub):
        c = remote(mine, sib.at[s], s_send.at[k], s_recv.at[k], dev(p, t, other(s, k, sub)))
        c.start()
        near.append(c)
    for c in near:
        c.wait_recv()
    total = sib[0]
    for k in range(1, sub):
        total = total + sib[k]
    held[...] = total
    far[p] = total
    for k in range(1, TEAM):
        c = remote(held, far.at[p], b_send.at[k], b_recv.at[k], dev(other(p, k, TEAM), t, s))
        c.start()
        second.append(c)
    for c in second:
        c.wait_recv()
    total = far[0]
    for k in range(1, TEAM):
        total = total + far[k]
    out_ref[t] = total
    for k in range(1, TEAM):
        c = remote(out_ref.at[t], out_ref.at[t], c_send.at[k], c_recv.at[k], dev(p, other(t, k, TEAM), s))
        c.start()
        third.append(c)
    for c in first + near + second:
        c.wait_send()
    for c in third:
        c.wait()


def small_sum(n, x):
    sub = n // (TEAM * TEAM)
    dma = pltpu.SemaphoreType.DMA
    tile = x.shape[1:]
    return pl.pallas_call(
        functools.partial(small_kernel, n),
        out_shape=jax.ShapeDtypeStruct(x.shape, F32),
        in_specs=[VMEM],
        out_specs=VMEM,
        scratch_shapes=[pltpu.VMEM((TEAM - 1,) + tile, F32), pltpu.VMEM(tile, F32), pltpu.VMEM((sub,) + tile, F32),
                        pltpu.VMEM(tile, F32), pltpu.VMEM((TEAM,) + tile, F32)]
        + [dma((TEAM,)), dma((TEAM,)), dma((sub,)), dma((sub,))] + [dma((TEAM,))] * 4,
        compiler_params=pltpu.CompilerParams(collective_id=5, has_side_effects=True),
        name="small_sum",
    )(x)


def gelu_tanh(inner):
    return jax.nn.gelu(inner, approximate=True)


def norm_back(inputs, scale, gain, upstream):
    weighted = gain * upstream
    return scale * weighted - inputs * scale * scale * scale * jnp.mean(
        weighted * inputs, axis=-1, keepdims=True
    )


def dot_t(a, b):
    return lax.dot_general(a, b, CONTRACT_COLS, preferred_element_type=F32)


def dot_r(a, b):
    return lax.dot_general(a, b, CONTRACT_ROWS, preferred_element_type=F32)


def dot(a, b):
    return jnp.dot(a, b, preferred_element_type=F32)


def body(n, tokens, attn_weight, w_gate, w_up, w_down, norm_gains, bias_table, router,
         grad_out, segment, expert_ids, bucket_of):
    rows, width = tokens.shape
    slots = bucket_of.shape[0]
    routed = router.shape[1]
    buckets, head_count = bias_table.shape
    head_width = width // head_count
    factor = head_width ** (-0.5)
    heads = head_count // TEAM
    part = heads * head_width
    sub, _, t, _, _ = place(n)
    all_rows = TEAM * rows
    spans = all_rows // slots

    early = jnp.stack([attn_weight.T, w_down])
    late = jnp.stack([w_gate.T, w_up.T])
    meta = jnp.concatenate([segment[None], expert_ids.T, jnp.zeros((5, rows), jnp.int32)], axis=0)
    w_all, tok_all, dy_all, meta_all = gather(n, early, tokens, grad_out, meta)
    w_all = w_all.reshape(2, -1, width)
    attn_t, down = w_all[0], w_all[1]
    qkv_t, out_t = attn_t[: 3 * part], attn_t[3 * part :]
    inputs = tok_all.reshape(all_rows, width).astype(F32)
    segments = meta_all[:, 0, :].reshape(all_rows)
    id_a = meta_all[:, 1, :].reshape(all_rows)
    id_b = meta_all[:, 2, :].reshape(all_rows)

    places = jnp.arange(slots)
    gap = places[:, None] - places[None, :]
    causal = gap >= 0
    gap_hit = (gap[:, :, None] == places[None, None, :]).astype(F32)
    bucket_hit = (bucket_of[:, None] == jnp.arange(buckets)[None, :]).astype(F32)
    table_mine = lax.dynamic_slice(bias_table, (0, heads * t), (buckets, heads))
    by_gap = jnp.dot(bucket_hit, table_mine, precision=HIGHEST)
    offsets = jnp.einsum("ijd,dh->hij", gap_hit, by_gap, precision=HIGHEST)

    scale_one = lax.rsqrt(jnp.mean(inputs * inputs, axis=-1, keepdims=True) + EPSILON)
    normed = (inputs * scale_one * norm_gains[0]).astype(BF16)
    triple = dot_t(normed, qkv_t).astype(BF16)
    heads_of = lambda v: v.reshape(spans, slots, heads, head_width)
    query = heads_of(triple[:, :part])
    keyset = heads_of(triple[:, part : 2 * part])
    valueset = heads_of(triple[:, 2 * part :])
    seg = segments.reshape(spans, slots)
    allowed = (seg[:, :, None] == seg[:, None, :]) & causal[None]
    raw = jnp.einsum("bihd,bjhd->bhij", query, keyset, preferred_element_type=F32)
    scores = jnp.where(allowed[:, None], raw * factor + offsets[None], -1e30)
    peak = jnp.max(scores, axis=-1, keepdims=True)
    lifted_scores = jnp.exp(scores - peak)
    weights = lifted_scores / jnp.sum(lifted_scores, axis=-1, keepdims=True)
    weights_low = weights.astype(BF16)
    mixed = jnp.einsum("bhij,bjhd->bihd", weights_low, valueset, preferred_element_type=F32)
    mixed = mixed.reshape(all_rows, part).astype(BF16)
    branch = dot(mixed, out_t).astype(BF16).reshape(TEAM, rows, width)
    middle, second_all, late_all = middle_exchange(n, branch, tokens, norm_gains, late)
    late_all = late_all.reshape(2, -1, width)
    gate_t, up_t = late_all[0], late_all[1]
    second_all = second_all.reshape(all_rows, width)

    second_wide = second_all.astype(F32)
    probs_all = jax.nn.softmax(jnp.dot(second_wide, router, precision=HIGHEST), axis=-1)
    lanes = jnp.arange(routed)[None, :]
    picked_all = jnp.where((id_a[:, None] == lanes) | (id_b[:, None] == lanes), 1.0, 0.0)
    total_all = jnp.sum(probs_all * picked_all, axis=-1)
    live_all = picked_all[:, 0] * jnp.where(segments >= 0, 1.0, 0.0)
    combine_all = probs_all[:, 0] * live_all / total_all
    gated = dot_t(second_all, gate_t)
    lifted = dot_t(second_all, up_t)
    activated, gelu_back = jax.vjp(gelu_tanh, gated)
    hidden = (activated * lifted).astype(BF16)
    out_part = dot(hidden, down).astype(BF16).reshape(TEAM, rows, width)
    d_expert = (combine_all[:, None] * dy_all.reshape(all_rows, width).astype(F32)).astype(BF16)
    d_hidden = dot_t(d_expert, down)
    d_gated = gelu_back(d_hidden * lifted)[0].astype(BF16)
    d_lifted = (d_hidden * activated).astype(BF16)
    back_part = (dot(d_gated, gate_t) + dot(d_lifted, up_t)).astype(BF16).reshape(TEAM, rows, width)
    grad_ffn = jnp.stack(
        [dot_r(d_gated, second_all).astype(BF16), dot_r(d_lifted, second_all).astype(BF16)]
    ).reshape(2, TEAM, sub, -1, width)
    (expert_out, d_second), _, g_ffn = reduce_exchange(n, (out_part, back_part), (), grad_ffn, 2)
    grad_down = dot_r(hidden, d_expert).astype(BF16).reshape(1, TEAM, sub, -1, width)

    mine = lambda v: lax.dynamic_slice_in_dim(v, t * rows, rows, 0)
    second, probs, picked = mine(second_wide), mine(probs_all), mine(picked_all)
    chosen_total, live, combine = mine(total_all), mine(live_all), mine(combine_all)
    upstream = grad_out.astype(F32)
    result = (middle + combine[:, None] * expert_out).astype(BF16)
    d_combine = jnp.sum(expert_out * upstream, axis=-1)
    first_hot = jnp.where(jnp.arange(routed) == 0, 1.0, 0.0)
    ratio = probs[:, 0] / (chosen_total * chosen_total)
    d_probs = (d_combine * live)[:, None] * (
        first_hot[None, :] / chosen_total[:, None] - ratio[:, None] * picked
    )
    d_logits = probs * (d_probs - jnp.sum(d_probs * probs, axis=-1, keepdims=True))
    grad_router_t = lax.dot_general(d_logits, second, CONTRACT_ROWS, precision=HIGHEST)
    d_second = d_second + jnp.dot(d_logits, router.T, precision=HIGHEST)
    scale_two = lax.rsqrt(jnp.mean(middle * middle, axis=-1, keepdims=True) + EPSILON)
    gain_two = jnp.sum(d_second * middle * scale_two, axis=0)
    d_middle = upstream + norm_back(middle, scale_two, norm_gains[1], d_second)
    _, (d_branch,), g_down = reduce_exchange(n, (), (d_middle.astype(BF16),), grad_down, 3)
    d_branch = d_branch.reshape(all_rows, width)

    grad_out_t = dot_r(mixed, d_branch)
    d_mixed = heads_of(dot_t(d_branch, out_t).astype(BF16))
    d_weights = jnp.einsum("bihd,bjhd->bhij", d_mixed, valueset, preferred_element_type=F32)
    d_values = jnp.einsum("bhij,bihd->bjhd", weights_low, d_mixed, preferred_element_type=F32)
    d_scores = weights * (d_weights - jnp.sum(weights * d_weights, axis=-1, keepdims=True))
    d_scores = d_scores.astype(BF16)
    d_query = jnp.einsum("bhij,bjhd->bihd", d_scores, keyset, preferred_element_type=F32) * factor
    d_keys = jnp.einsum("bhij,bihd->bjhd", d_scores, query, preferred_element_type=F32) * factor
    score_sum = jnp.sum(d_scores.astype(F32), axis=0)
    gap_sum = jnp.einsum("hij,ijd->dh", score_sum, gap_hit, precision=HIGHEST)
    table_part = lax.dot_general(bucket_hit, gap_sum, CONTRACT_ROWS, precision=HIGHEST)
    grad_table = lax.dynamic_update_slice(jnp.zeros(bias_table.shape, F32), table_part, (0, heads * t))
    flat = lambda v: v.reshape(all_rows, part).astype(BF16)
    d_triple = jnp.concatenate([flat(d_query), flat(d_keys), flat(d_values)], axis=1)
    grad_in_t = dot_r(d_triple, normed)
    grad_attn = jnp.concatenate([grad_in_t, grad_out_t], axis=0).astype(BF16)
    grad_attn = grad_attn.reshape(1, TEAM, sub, -1, width)
    d_normed_part = dot(d_triple, qkv_t).astype(BF16).reshape(TEAM, rows, width)
    (d_normed,), _, g_attn = reduce_exchange(n, (d_normed_part,), (), grad_attn, 4)

    own_inputs = tokens.astype(F32)
    own_scale = mine(scale_one)
    gain_one = jnp.sum(d_normed * own_inputs * own_scale, axis=0)
    input_grad = (d_middle + norm_back(own_inputs, own_scale, norm_gains[0], d_normed)).astype(BF16)
    table_flat = grad_table.reshape(-1)
    lines = -(-table_flat.shape[0] // width)
    table_rows = jnp.pad(table_flat, (0, lines * width - table_flat.shape[0])).reshape(lines, width)
    small = jnp.concatenate([grad_router_t, gain_one[None], gain_two[None], table_rows], axis=0)
    depth = -(-small.shape[0] // (8 * TEAM)) * 8
    small = jnp.pad(small, ((0, depth * TEAM - small.shape[0]), (0, 0))).reshape(TEAM, depth, width)
    small = small_sum(n, small).reshape(TEAM * depth, width)
    grad_router = small[:routed].T
    grad_gains = small[routed : routed + 2]
    grad_table = small[routed + 2 : routed + 2 + lines].reshape(-1)[: table_flat.shape[0]].reshape(bias_table.shape)
    return (result, input_grad, g_attn[0].T, g_ffn[0].T, g_ffn[1].T, g_down[0],
            grad_gains, grad_table, grad_router)


def solution(mesh):
    n = mesh.shape["fsdp"]
    row, col = P("fsdp", None), P(None, "fsdp")
    in_specs = (row, col, col, col, row, P(), P(), P(), row, P("fsdp"), row, P())
    out_specs = (row, row, col, col, col, row, P(), P(), P())
    return jax.shard_map(
        functools.partial(body, n), mesh=mesh, in_specs=in_specs, out_specs=out_specs, check_vma=False
    )
```

```python
import functools
import jax
import jax.numpy as jnp
from jax import lax
from jax.experimental import pallas as pl
from jax.experimental.pallas import tpu as pltpu
from jax.sharding import PartitionSpec as P

EPSILON = 1e-06
HIGHEST = lax.Precision.HIGHEST
MESH = pl.DeviceIdType.MESH
TEAM = 4
F32 = jnp.float32
BF16 = jnp.bfloat16
VMEM = pl.BlockSpec(memory_space=pltpu.VMEM)
ANY = pl.BlockSpec(memory_space=pl.ANY)
CONTRACT_ROWS = (((0,), (0,)), ((), ()))
CONTRACT_COLS = (((1,), (1,)), ((), ()))


def place(n):
    sub = n // (TEAM * TEAM)
    me = lax.axis_index("fsdp")
    p = me // (TEAM * sub)
    t = lax.rem(me // sub, TEAM)
    s = lax.rem(me, sub)
    return sub, p, t, s, (lambda p, t, s: (p * (TEAM * sub) + t * sub + s,))


def greet(peers):
    barrier = pltpu.get_barrier_semaphore()
    for peer in peers:
        pl.semaphore_signal(barrier, inc=1, device_id=peer, device_id_type=MESH)
    pl.semaphore_wait(barrier, len(peers))


def remote(src, dst, send, recv, peer):
    return pltpu.make_async_remote_copy(
        src_ref=src, dst_ref=dst, send_sem=send, recv_sem=recv, device_id=peer, device_id_type=MESH
    )


def other(index, step, count):
    return lax.rem(index + step, count)


def spread_peers(sub, p, t, s, dev):
    peers = [dev(other(p, k, TEAM), t, s) for k in range(1, TEAM)]
    return peers + [dev(p, t, other(s, k, sub)) for k in range(1, sub)]


def team_peers(p, t, s, dev):
    return [dev(p, other(t, k, TEAM), s) for k in range(1, TEAM)]


def weights_start(n, w_ref, w_all, sems):
    sub, p, t, s, dev = place(n)
    p_send, p_recv, s_send, s_recv, own_sem = sems
    wide, near, local = [], [], []
    for i in range(w_ref.shape[0]):
        for k in range(1, TEAM):
            c = remote(w_ref.at[i], w_all.at[i, p, s], p_send.at[i, k], p_recv.at[i, k],
                       dev(other(p, k, TEAM), t, s))
            c.start()
            wide.append(c)
    for i in range(w_ref.shape[0]):
        for k in range(1, sub):
            c = remote(w_ref.at[i], w_all.at[i, p, s], s_send.at[i, 0, k], s_recv.at[i, 0, k],
                       dev(p, t, other(s, k, sub)))
            c.start()
            near.append(c)
        c = pltpu.make_async_copy(w_ref.at[i], w_all.at[i, p, s], own_sem.at[i])
        c.start()
        local.append(c)
    return wide, near, local


def weights_finish(n, w_all, sems, state):
    sub, p, t, s, dev = place(n)
    _, _, s_send, s_recv, _ = sems
    wide, near, local = state
    for i in range(w_all.shape[0]):
        for k in range(1, TEAM):
            wide[i * (TEAM - 1) + k - 1].wait_recv()
            q = other(p, TEAM - k, TEAM)
            for j in range(1, sub):
                c = remote(w_all.at[i, q, s], w_all.at[i, q, s], s_send.at[i, k, j], s_recv.at[i, k, j],
                           dev(p, t, other(s, j, sub)))
                c.start()
                near.append(c)
    for c in wide:
        c.wait_send()
    for c in near:
        c.wait()
    for c in local:
        c.wait()


def weights_sems(n, kinds):
    sub = n // (TEAM * TEAM)
    dma = pltpu.SemaphoreType.DMA
    return [dma((kinds, TEAM)), dma((kinds, TEAM)), dma((kinds, TEAM, sub)), dma((kinds, TEAM, sub)), dma((kinds,))]


def weights_shape(n, w):
    return jax.ShapeDtypeStruct((w.shape[0], TEAM, n // (TEAM * TEAM)) + w.shape[1:], w.dtype)


def gather_kernel(n, w_ref, tok_ref, dy_ref, meta_ref, w_all, tok_all, dy_all, meta_all,
                  t_send, t_recv, own_sem, *sems):
    sub, p, t, s, dev = place(n)
    greet(spread_peers(sub, p, t, s, dev) + team_peers(p, t, s, dev))
    state = weights_start(n, w_ref, w_all, sems)
    copies, local = [], []
    for i, (src, dst) in enumerate(((tok_ref, tok_all), (dy_ref, dy_all), (meta_ref, meta_all))):
        for k in range(1, TEAM):
            c = remote(src, dst.at[t], t_send.at[i, k], t_recv.at[i, k], dev(p, other(t, k, TEAM), s))
            c.start()
            copies.append(c)
        c = pltpu.make_async_copy(src, dst.at[t], own_sem.at[i])
        c.start()
        local.append(c)
    weights_finish(n, w_all, sems, state)
    for c in copies:
        c.wait()
    for c in local:
        c.wait()


def gather(n, w, tok, dy, meta):
    dma = pltpu.SemaphoreType.DMA
    shape = jax.ShapeDtypeStruct
    return pl.pallas_call(
        functools.partial(gather_kernel, n),
        out_shape=(
            weights_shape(n, w),
            shape((TEAM,) + tok.shape, BF16),
            shape((TEAM,) + dy.shape, BF16),
            shape((TEAM,) + meta.shape, jnp.int32),
        ),
        in_specs=[VMEM] * 4,
        out_specs=(ANY,) * 4,
        scratch_shapes=[dma((3, TEAM)), dma((3, TEAM)), dma((3,))] + weights_sems(n, w.shape[0]),
        compiler_params=pltpu.CompilerParams(collective_id=0, has_side_effects=True),
        name="gather_all",
    )(w, tok, dy, meta)


def middle_kernel(n, part_ref, x_ref, gain_ref, w_ref, y_ref, h_all, w_all, got, held,
                  a_send, a_recv, b_send, b_recv, own_sem, *sems):
    sub, p, t, s, dev = place(n)
    greet(spread_peers(sub, p, t, s, dev) + team_peers(p, t, s, dev))
    copies = []
    for k in range(1, TEAM):
        u = other(t, k, TEAM)
        c = remote(part_ref.at[u], got.at[k - 1], a_send.at[k], a_recv.at[k], dev(p, u, s))
        c.start()
        copies.append(c)
    state = weights_start(n, w_ref, w_all, sems)
    total = x_ref[...].astype(F32) + part_ref[t].astype(F32)
    for k in range(1, TEAM):
        copies[k - 1].wait_recv()
        total = total + got[k - 1].astype(F32)
    y_ref[...] = total
    scale = lax.rsqrt(jnp.mean(total * total, axis=-1, keepdims=True) + EPSILON)
    held[...] = (total * scale * gain_ref[1:2, :]).astype(BF16)
    local = pltpu.make_async_copy(held, h_all.at[t], own_sem)
    local.start()
    sends = []
    for k in range(1, TEAM):
        c = remote(held, h_all.at[t], b_send.at[k], b_recv.at[k], dev(p, other(t, k, TEAM), s))
        c.start()
        sends.append(c)
    weights_finish(n, w_all, sems, state)
    for c in copies:
        c.wait_send()
    for c in sends:
        c.wait()
    local.wait()


def middle_exchange(n, part, x, gains, w):
    dma = pltpu.SemaphoreType.DMA
    shape = jax.ShapeDtypeStruct
    return pl.pallas_call(
        functools.partial(middle_kernel, n),
        out_shape=(shape(x.shape, F32), shape((TEAM,) + x.shape, BF16), weights_shape(n, w)),
        in_specs=[VMEM] * 4,
        out_specs=(VMEM, ANY, ANY),
        scratch_shapes=[pltpu.VMEM((TEAM - 1,) + x.shape, BF16), pltpu.VMEM(x.shape, BF16),
                        dma((TEAM,)), dma((TEAM,)), dma((TEAM,)), dma((TEAM,)), dma] + weights_sems(n, w.shape[0]),
        compiler_params=pltpu.CompilerParams(collective_id=1, has_side_effects=True),
        name="middle_exchange",
    )(part, x, gains, w)


def reduce_kernel(n, m, h, gain_row, *refs):
    parts, rows, grad_ref = refs[:m], refs[m:m + h], refs[m + h]
    refs = refs[m + h + 1:]
    small = gain_row is not None
    if small:
        unit_ref, small_ref = refs[:2]
        refs = refs[2:]
    outs, rows_all, grad_out = refs[:m], refs[m:m + h], refs[m + h]
    if small:
        small_out = refs[m + h + 1]
        refs = refs[:m + h + 1] + refs[m + h + 2:]
    (got, sib, to_send, far, t_send, t_recv, h_send, h_recv, own_sem,
     s_send, s_recv, p_send, p_recv) = refs[m + h + 1:m + h + 14]
    rest = refs[m + h + 14:]
    sub, p, t, s, dev = place(n)
    greet(spread_peers(sub, p, t, s, dev) + team_peers(p, t, s, dev))
    kinds = grad_ref.shape[0]
    near, tokens, wide, shared, local = [], [], [], [], []
    for kind in range(kinds):
        for k in range(1, sub):
            v = other(s, k, sub)
            c = remote(grad_ref.at[kind, :, v], sib.at[kind, k - 1], s_send.at[kind, k], s_recv.at[kind, k],
                       dev(p, t, v))
            c.start()
            near.append(c)
    for i in range(h):
        for k in range(1, TEAM):
            c = remote(rows[i], rows_all[i].at[t], h_send.at[i, k], h_recv.at[i, k],
                       dev(p, other(t, k, TEAM), s))
            c.start()
            shared.append(c)
        c = pltpu.make_async_copy(rows[i], rows_all[i].at[t], own_sem.at[i])
        c.start()
        local.append(c)
    for i in range(m):
        for k in range(1, TEAM):
            u = other(t, k, TEAM)
            c = remote(parts[i].at[u], got.at[i, k - 1], t_send.at[i, k], t_recv.at[i, k], dev(p, u, s))
            c.start()
            tokens.append(c)
    for kind in range(kinds):
        for c in near[kind * (sub - 1):(kind + 1) * (sub - 1)]:
            c.wait_recv()
        for k in range(1, TEAM):
            q = other(p, k, TEAM)
            total = grad_ref[kind, q, s].astype(F32)
            for j in range(1, sub):
                total = total + sib[kind, j - 1, q].astype(F32)
            to_send[kind, k - 1] = total.astype(BF16)
            c = remote(to_send.at[kind, k - 1], far.at[kind, k - 1], p_send.at[kind, k], p_recv.at[kind, k],
                       dev(q, t, s))
            c.start()
            wide.append(c)
    for i in range(m):
        total = parts[i][t].astype(F32)
        for k in range(1, TEAM):
            tokens[i * (TEAM - 1) + k - 1].wait_recv()
            total = total + got[i, k - 1].astype(F32)
        outs[i][...] = total
    if small:
        buf = rest[0]
        piece, line = divmod(gain_row, small_ref.shape[1])
        gain = jnp.sum(outs[0][...] * unit_ref[...], axis=0, keepdims=True)
        buf[...] = small_ref[...]
        buf[piece, line:line + 1, :] = gain
        small_phases(n, buf, small_out, *rest[1:])
    for kind in range(kinds):
        for c in wide[kind * (TEAM - 1):(kind + 1) * (TEAM - 1)]:
            c.wait_recv()
        total = grad_ref[kind, p, s].astype(F32)
        for j in range(1, sub):
            total = total + sib[kind, j - 1, p].astype(F32)
        for k in range(1, TEAM):
            total = total + far[kind, k - 1].astype(F32)
        grad_out[kind] = total
    for c in near + tokens + wide:
        c.wait_send()
    for c in shared:
        c.wait()
    for c in local:
        c.wait()


def reduce_exchange(n, parts, rows, grads, ident, small=(), gain_row=None):
    sub = n // (TEAM * TEAM)
    m, h = len(parts), len(rows)
    dma = pltpu.SemaphoreType.DMA
    shape = jax.ShapeDtypeStruct
    block = parts[0].shape[1:] if m else (8, 128)
    kinds, tile = grads.shape[0], grads.shape[3:]
    outs = pl.pallas_call(
        functools.partial(reduce_kernel, n, m, h, gain_row),
        out_shape=(shape(block, F32),) * m
        + tuple(shape((TEAM,) + v.shape, v.dtype) for v in rows)
        + (shape((kinds,) + tile, F32),)
        + tuple(shape(v.shape, F32) for v in small[1:]),
        in_specs=[VMEM] * (m + h + 1 + len(small)),
        out_specs=(VMEM,) * m + (ANY,) * h + (VMEM,) * (1 + len(small[1:])),
        scratch_shapes=[
            pltpu.VMEM((max(m, 1), TEAM - 1) + block, BF16),
            pltpu.VMEM((kinds, sub - 1, TEAM) + tile, BF16),
            pltpu.VMEM((kinds, TEAM - 1) + tile, BF16),
            pltpu.VMEM((kinds, TEAM - 1) + tile, BF16),
            dma((max(m, 1), TEAM)), dma((max(m, 1), TEAM)),
            dma((max(h, 1), TEAM)), dma((max(h, 1), TEAM)), dma((max(h, 1),)),
            dma((kinds, sub)), dma((kinds, sub)), dma((kinds, TEAM)), dma((kinds, TEAM)),
        ] + (small_scratch(n, small[1].shape) if small else []),
        compiler_params=pltpu.CompilerParams(collective_id=ident, has_side_effects=True),
        name=f"reduce_{ident}",
    )(*parts, *rows, grads, *small)
    return (outs[:m], outs[m:m + h]) + tuple(outs[m + h:])


def small_phases(n, buf, out_ref, got, mine, sib, held, far,
                 a_send, a_recv, s_send, s_recv, b_send, b_recv, c_send, c_recv):
    sub, p, t, s, dev = place(n)
    first, near, second, third = [], [], [], []
    for k in range(1, TEAM):
        u = other(t, k, TEAM)
        c = remote(buf.at[u], got.at[k - 1], a_send.at[k], a_recv.at[k], dev(p, u, s))
        c.start()
        first.append(c)
    total = buf[t]
    for k in range(1, TEAM):
        first[k - 1].wait_recv()
        total = total + got[k - 1]
    mine[...] = total
    sib[s] = total
    for k in range(1, sub):
        c = remote(mine, sib.at[s], s_send.at[k], s_recv.at[k], dev(p, t, other(s, k, sub)))
        c.start()
        near.append(c)
    for c in near:
        c.wait_recv()
    total = sib[0]
    for k in range(1, sub):
        total = total + sib[k]
    held[...] = total
    far[p] = total
    for k in range(1, TEAM):
        c = remote(held, far.at[p], b_send.at[k], b_recv.at[k], dev(other(p, k, TEAM), t, s))
        c.start()
        second.append(c)
    for c in second:
        c.wait_recv()
    total = far[0]
    for k in range(1, TEAM):
        total = total + far[k]
    out_ref[t] = total
    for k in range(1, TEAM):
        c = remote(out_ref.at[t], out_ref.at[t], c_send.at[k], c_recv.at[k], dev(p, other(t, k, TEAM), s))
        c.start()
        third.append(c)
    for c in first + near + second:
        c.wait_send()
    for c in third:
        c.wait()


def small_scratch(n, shape):
    sub = n // (TEAM * TEAM)
    dma = pltpu.SemaphoreType.DMA
    tile = shape[1:]
    return [pltpu.VMEM(shape, F32), pltpu.VMEM((TEAM - 1,) + tile, F32), pltpu.VMEM(tile, F32),
            pltpu.VMEM((sub,) + tile, F32), pltpu.VMEM(tile, F32), pltpu.VMEM((TEAM,) + tile, F32),
            dma((TEAM,)), dma((TEAM,)), dma((sub,)), dma((sub,))] + [dma((TEAM,))] * 4


def gelu_tanh(inner):
    return jax.nn.gelu(inner, approximate=True)


def norm_back(inputs, scale, gain, upstream):
    weighted = gain * upstream
    return scale * weighted - inputs * scale * scale * scale * jnp.mean(
        weighted * inputs, axis=-1, keepdims=True
    )


def dot_t(a, b):
    return lax.dot_general(a, b, CONTRACT_COLS, preferred_element_type=F32)


def dot_r(a, b):
    return lax.dot_general(a, b, CONTRACT_ROWS, preferred_element_type=F32)


def dot(a, b):
    return jnp.dot(a, b, preferred_element_type=F32)


def body(n, tokens, attn_weight, w_gate, w_up, w_down, norm_gains, bias_table, router,
         grad_out, segment, expert_ids, bucket_of):
    rows, width = tokens.shape
    slots = bucket_of.shape[0]
    routed = router.shape[1]
    buckets, head_count = bias_table.shape
    head_width = width // head_count
    factor = head_width ** (-0.5)
    heads = head_count // TEAM
    part = heads * head_width
    sub, _, t, _, _ = place(n)
    all_rows = TEAM * rows
    spans = all_rows // slots

    early = jnp.stack([attn_weight.T, w_down])
    late = jnp.stack([w_gate.T, w_up.T])
    meta = jnp.concatenate([segment[None], expert_ids.T, jnp.zeros((5, rows), jnp.int32)], axis=0)
    w_all, tok_all, dy_all, meta_all = gather(n, early, tokens, grad_out, meta)
    w_all = w_all.reshape(2, -1, width)
    attn_t, down = w_all[0], w_all[1]
    qkv_t, out_t = attn_t[: 3 * part], attn_t[3 * part :]
    inputs = tok_all.reshape(all_rows, width).astype(F32)
    segments = meta_all[:, 0, :].reshape(all_rows)
    id_a = meta_all[:, 1, :].reshape(all_rows)
    id_b = meta_all[:, 2, :].reshape(all_rows)

    places = jnp.arange(slots)
    gap = places[:, None] - places[None, :]
    causal = gap >= 0
    gap_hit = (gap[:, :, None] == places[None, None, :]).astype(F32)
    bucket_hit = (bucket_of[:, None] == jnp.arange(buckets)[None, :]).astype(F32)
    table_mine = lax.dynamic_slice(bias_table, (0, heads * t), (buckets, heads))
    by_gap = jnp.dot(bucket_hit, table_mine, precision=HIGHEST)
    offsets = jnp.einsum("ijd,dh->hij", gap_hit, by_gap, precision=HIGHEST)

    scale_one = lax.rsqrt(jnp.mean(inputs * inputs, axis=-1, keepdims=True) + EPSILON)
    normed = (inputs * scale_one * norm_gains[0]).astype(BF16)
    triple = dot_t(normed, qkv_t).astype(BF16)
    heads_of = lambda v: v.reshape(spans, slots, heads, head_width)
    query = heads_of(triple[:, :part])
    keyset = heads_of(triple[:, part : 2 * part])
    valueset = heads_of(triple[:, 2 * part :])
    seg = segments.reshape(spans, slots)
    allowed = (seg[:, :, None] == seg[:, None, :]) & causal[None]
    raw = jnp.einsum("bihd,bjhd->bhij", query, keyset, preferred_element_type=F32)
    scores = jnp.where(allowed[:, None], raw * factor + offsets[None], -1e30)
    peak = jnp.max(scores, axis=-1, keepdims=True)
    lifted_scores = jnp.exp(scores - peak)
    weights = lifted_scores / jnp.sum(lifted_scores, axis=-1, keepdims=True)
    weights_low = weights.astype(BF16)
    mixed = jnp.einsum("bhij,bjhd->bihd", weights_low, valueset, preferred_element_type=F32)
    mixed = mixed.reshape(all_rows, part).astype(BF16)
    branch = dot(mixed, out_t).astype(BF16).reshape(TEAM, rows, width)
    middle, second_all, late_all = middle_exchange(n, branch, tokens, norm_gains, late)
    late_all = late_all.reshape(2, -1, width)
    gate_t, up_t = late_all[0], late_all[1]
    second_all = second_all.reshape(all_rows, width)

    second_wide = second_all.astype(F32)
    probs_all = jax.nn.softmax(jnp.dot(second_wide, router, precision=HIGHEST), axis=-1)
    lanes = jnp.arange(routed)[None, :]
    picked_all = jnp.where((id_a[:, None] == lanes) | (id_b[:, None] == lanes), 1.0, 0.0)
    total_all = jnp.sum(probs_all * picked_all, axis=-1)
    live_all = picked_all[:, 0] * jnp.where(segments >= 0, 1.0, 0.0)
    combine_all = probs_all[:, 0] * live_all / total_all
    gated = dot_t(second_all, gate_t)
    lifted = dot_t(second_all, up_t)
    activated, gelu_back = jax.vjp(gelu_tanh, gated)
    hidden = (activated * lifted).astype(BF16)
    out_part = dot(hidden, down).astype(BF16).reshape(TEAM, rows, width)
    d_expert = (combine_all[:, None] * dy_all.reshape(all_rows, width).astype(F32)).astype(BF16)
    d_hidden = dot_t(d_expert, down)
    d_gated = gelu_back(d_hidden * lifted)[0].astype(BF16)
    d_lifted = (d_hidden * activated).astype(BF16)
    back_part = (dot(d_gated, gate_t) + dot(d_lifted, up_t)).astype(BF16).reshape(TEAM, rows, width)
    grad_ffn = jnp.stack(
        [dot_r(d_gated, second_all).astype(BF16), dot_r(d_lifted, second_all).astype(BF16)]
    ).reshape(2, TEAM, sub, -1, width)
    (expert_out, d_second), _, g_ffn = reduce_exchange(n, (out_part, back_part), (), grad_ffn, 2)
    grad_down = dot_r(hidden, d_expert).astype(BF16).reshape(1, TEAM, sub, -1, width)

    mine = lambda v: lax.dynamic_slice_in_dim(v, t * rows, rows, 0)
    second, probs, picked = mine(second_wide), mine(probs_all), mine(picked_all)
    chosen_total, live, combine = mine(total_all), mine(live_all), mine(combine_all)
    upstream = grad_out.astype(F32)
    result = (middle + combine[:, None] * expert_out).astype(BF16)
    d_combine = jnp.sum(expert_out * upstream, axis=-1)
    first_hot = jnp.where(jnp.arange(routed) == 0, 1.0, 0.0)
    ratio = probs[:, 0] / (chosen_total * chosen_total)
    d_probs = (d_combine * live)[:, None] * (
        first_hot[None, :] / chosen_total[:, None] - ratio[:, None] * picked
    )
    d_logits = probs * (d_probs - jnp.sum(d_probs * probs, axis=-1, keepdims=True))
    grad_router_t = lax.dot_general(d_logits, second, CONTRACT_ROWS, precision=HIGHEST)
    d_second = d_second + jnp.dot(d_logits, router.T, precision=HIGHEST)
    scale_two = lax.rsqrt(jnp.mean(middle * middle, axis=-1, keepdims=True) + EPSILON)
    gain_two = jnp.sum(d_second * middle * scale_two, axis=0)
    d_middle = upstream + norm_back(middle, scale_two, norm_gains[1], d_second)
    _, (d_branch,), g_down = reduce_exchange(n, (), (d_middle.astype(BF16),), grad_down, 3)
    d_branch = d_branch.reshape(all_rows, width)

    grad_out_t = dot_r(mixed, d_branch)
    d_mixed = heads_of(dot_t(d_branch, out_t).astype(BF16))
    d_weights = jnp.einsum("bihd,bjhd->bhij", d_mixed, valueset, preferred_element_type=F32)
    d_values = jnp.einsum("bhij,bihd->bjhd", weights_low, d_mixed, preferred_element_type=F32)
    d_scores = weights * (d_weights - jnp.sum(weights * d_weights, axis=-1, keepdims=True))
    d_scores = d_scores.astype(BF16)
    d_query = jnp.einsum("bhij,bjhd->bihd", d_scores, keyset, preferred_element_type=F32) * factor
    d_keys = jnp.einsum("bhij,bihd->bjhd", d_scores, query, preferred_element_type=F32) * factor
    score_sum = jnp.sum(d_scores.astype(F32), axis=0)
    gap_sum = jnp.einsum("hij,ijd->dh", score_sum, gap_hit, precision=HIGHEST)
    table_part = lax.dot_general(bucket_hit, gap_sum, CONTRACT_ROWS, precision=HIGHEST)
    grad_table = lax.dynamic_update_slice(jnp.zeros(bias_table.shape, F32), table_part, (0, heads * t))
    flat = lambda v: v.reshape(all_rows, part).astype(BF16)
    d_triple = jnp.concatenate([flat(d_query), flat(d_keys), flat(d_values)], axis=1)
    grad_in_t = dot_r(d_triple, normed)
    grad_attn = jnp.concatenate([grad_in_t, grad_out_t], axis=0).astype(BF16)
    grad_attn = grad_attn.reshape(1, TEAM, sub, -1, width)
    d_normed_part = dot(d_triple, qkv_t).astype(BF16).reshape(TEAM, rows, width)
    own_inputs = tokens.astype(F32)
    own_scale = mine(scale_one)
    table_flat = grad_table.reshape(-1)
    lines = -(-table_flat.shape[0] // width)
    table_rows = jnp.pad(table_flat, (0, lines * width - table_flat.shape[0])).reshape(lines, width)
    small = jnp.concatenate([grad_router_t, jnp.zeros((1, width), F32), gain_two[None], table_rows], axis=0)
    depth = -(-small.shape[0] // (8 * TEAM)) * 8
    small = jnp.pad(small, ((0, depth * TEAM - small.shape[0]), (0, 0))).reshape(TEAM, depth, width)
    (d_normed,), _, g_attn, small = reduce_exchange(
        n, (d_normed_part,), (), grad_attn, 4, (own_inputs * own_scale, small), routed
    )
    small = small.reshape(TEAM * depth, width)
    input_grad = (d_middle + norm_back(own_inputs, own_scale, norm_gains[0], d_normed)).astype(BF16)
    grad_router = small[:routed].T
    grad_gains = small[routed : routed + 2]
    grad_table = small[routed + 2 : routed + 2 + lines].reshape(-1)[: table_flat.shape[0]].reshape(bias_table.shape)
    return (result, input_grad, g_attn[0].T, g_ffn[0].T, g_ffn[1].T, g_down[0],
            grad_gains, grad_table, grad_router)


def solution(mesh):
    n = mesh.shape["fsdp"]
    row, col = P("fsdp", None), P(None, "fsdp")
    in_specs = (row, col, col, col, row, P(), P(), P(), row, P("fsdp"), row, P())
    out_specs = (row, row, col, col, col, row, P(), P(), P())
    return jax.shard_map(
        functools.partial(body, n), mesh=mesh, in_specs=in_specs, out_specs=out_specs, check_vma=False
    )
```
